32 devices in a mesh: dp: 8 (over z, x), rep: 4 (over y, core).
Axes of the slice: x: 2, y: 2, z: 4, core: 2. Of those that a mesh axis runs over, the one named last changes fastest.
Arguments:
- grad: bfloat16 [8, 512, 512], P(None, 'dp'), may hold values from -6 to 6
- block_slot: int32 [8], replicated, may hold values from 0 to 15, as said below
- left_stat: float32 [16, 512, 512], P('dp', 'rep'), may hold values from -6 to 6
- right_stat: float32 [16, 512, 512], P('dp', 'rep'), may hold values from -6 to 6
- left_root: bfloat16 [16, 512, 512], P('dp')
- right_root: bfloat16 [16, 512, 512], P('dp')
- graft_acc: float32 [16, 512, 512], P('dp'), may hold values from 0.25 to 4
Outputs:
- update: bfloat16 [8, 512, 512], P(None, 'dp', 'rep')
- new_left: float32 [16, 512, 512], P('dp', 'rep')
- new_right: float32 [16, 512, 512], P('dp', 'rep')
- new_graft: float32 [16, 512, 512], P('dp')
The draws below stay inside these ranges and needn't reach their ends.
Inputs may be any that keep to these rules, and one draw needn't show every extreme that they name: `block_slot`: distinct slot numbers; slot s belongs to owner s // 2, an index of dp, so an owner holds at most 2 blocks, and some owner holds exactly 2.
All inputs are finite; a program needn't handle non-finite values.
Results may differ from the reference program's by a relative error of at most 0.0049.
Values may be sent and summed in bfloat16 or wider, within the bound.
A program may use at most 64 MiB of HBM per device.

```python
import math
import jax
import jax.numpy as jnp
from jax import lax

BLK = 512
BMAX = 2
NB = 8
SLOTS = 16


def draw_block_slot(key, part):
    first_key, second_key, third_key = jax.random.split(jax.random.fold_in(key, 11), 3)
    full_owner = jax.random.randint(first_key, (), 0, SLOTS // BMAX)
    position = jnp.arange(SLOTS, dtype=jnp.int32)
    scores = jax.random.permutation(second_key, SLOTS).astype(jnp.int32) + BMAX
    scores = jnp.where(position // BMAX == full_owner, position % BMAX, scores)
    ranked = jnp.argsort(scores)
    chosen = ranked[:NB].astype(jnp.int32)
    shuffle = jax.random.permutation(third_key, NB)
    return chosen[shuffle].astype(jnp.int32)


def draw_left_root(key, part):
    first_key, second_key = jax.random.split(jax.random.fold_in(key, 21))
    upper = 10.0
    entries = jax.random.normal(first_key, (SLOTS, BLK, BLK), jnp.float32) / math.sqrt(BLK)
    log_scales = jax.random.uniform(second_key, (SLOTS, BLK, 1), jnp.float32, 0.0, math.log(upper))
    return (entries * jnp.exp(log_scales)).astype(jnp.bfloat16)


def draw_right_root(key, part):
    first_key, second_key = jax.random.split(jax.random.fold_in(key, 31))
    upper = 10.0
    entries = jax.random.normal(first_key, (SLOTS, BLK, BLK), jnp.float32) / math.sqrt(BLK)
    trend = math.log(3.0) * jnp.arange(BLK, dtype=jnp.float32) / BLK
    log_scales = jax.random.uniform(second_key, (SLOTS, 1, BLK), jnp.float32, 0.0, math.log(upper)) + trend[None, None, :]
    return (entries * jnp.exp(log_scales)).astype(jnp.bfloat16)


def block_levels(rng, dims, shards, low, top_value):
    factor_of = 1.0
    for dim, shards_of in shards:
        heights = jax.random.uniform(jax.random.fold_in(jax.random.fold_in(rng, 6), dim), (shards_of,), jnp.float32, low / len(shards), top_value / len(shards))
        factor_of = factor_of * jnp.repeat(jnp.exp(heights), dims[dim] // shards_of).reshape((-1,) + (1,) * (len(dims) - 1 - dim))
    return factor_of


def bell_draw(stream_key, dims, width, most, shards=(), kind=jnp.bfloat16):
    values = width * jax.random.normal(stream_key, dims, jnp.float32)
    if shards:
        values = values * block_levels(stream_key, dims, shards, -0.22, 0.18)
    return jnp.clip(values, -most, most).astype(kind)


def setup_inputs(seed: int = 0) -> dict:
    seeds = jax.random.split(jax.random.key(seed), 8)
    grad = bell_draw(seeds[0], (NB, BLK, BLK), 1.0, 6.0, ((1, 8),))
    block_slot = draw_block_slot(jax.random.fold_in(seeds[7], 71), 0)
    left_stat = bell_draw(seeds[2], (SLOTS, BLK, BLK), 1.0, 6.0, ((0, 8), (1, 4)), jnp.float32)
    right_stat = bell_draw(seeds[3], (SLOTS, BLK, BLK), 1.0, 6.0, ((0, 8), (1, 4)), jnp.float32)
    left_root = draw_left_root(jax.random.fold_in(seeds[7], 71), 0)
    right_root = draw_right_root(jax.random.fold_in(seeds[7], 71), 0)
    graft_acc = jnp.clip(jnp.exp(math.log(4.0) - 2.7725887 * jax.random.uniform(seeds[6], (SLOTS, BLK, BLK), jnp.float32) ** block_levels(seeds[6], (SLOTS, BLK, BLK), ((0, 8),), -0.2, 0.2)), 0.25, 4.0)
    return {"grad": grad, "block_slot": block_slot, "left_stat": left_stat, "right_stat": right_stat, "left_root": left_root, "right_root": right_root, "graft_acc": graft_acc}


decay_rate = 0.99
epsilon = 1e-06

def one_slot(members):
    grad_block, left_old, right_old, left_inv, right_inv, graft_old = members
    left_new = decay_rate * left_old + (1.0 - decay_rate) * jnp.dot(grad_block, grad_block.T, preferred_element_type=jnp.float32)
    right_new = decay_rate * right_old + (1.0 - decay_rate) * jnp.dot(grad_block.T, grad_block, preferred_element_type=jnp.float32)
    widened = grad_block.astype(jnp.float32)
    graft_new = decay_rate * graft_old + (1.0 - decay_rate) * widened * widened
    direction = widened / (jnp.sqrt(graft_new) + epsilon)
    middle = jnp.dot(grad_block, right_inv, preferred_element_type=jnp.float32).astype(jnp.bfloat16)
    precond = jnp.dot(left_inv, middle, preferred_element_type=jnp.float32)
    graft_scale = jnp.sqrt(jnp.sum(direction * direction)) / (jnp.sqrt(jnp.sum(precond * precond)) + epsilon)
    updates = (graft_scale * precond).astype(jnp.bfloat16)
    return (left_new, right_new, graft_new, updates)

def reference(grad, block_slot, left_stat, right_stat, left_root, right_root, graft_acc):
    slot_count = left_stat.shape[0]
    placed = jnp.zeros((slot_count, BLK, BLK), jnp.bfloat16).at[block_slot.astype(jnp.int32)].set(grad)
    left_new, right_new, graft_new, updates = lax.map(one_slot, (placed, left_stat, right_stat, left_root, right_root, graft_acc))
    update = updates[block_slot.astype(jnp.int32)]
    return (update, left_new, right_new, graft_new)
```

```python
import functools

import jax
import jax.numpy as jnp
from jax import lax
from jax.experimental import pallas as pl
from jax.experimental.pallas import tpu as pltpu
from jax.sharding import PartitionSpec as P

decay_rate = 0.99
epsilon = 1e-06


def local_plain(grad, block_slot, left_stat, right_stat, left_root, right_root, graft_acc):
    owners = lax.axis_size("dp")
    replicas = lax.axis_size("rep")
    blocks, band_rows, block_size = grad.shape
    capacity = left_stat.shape[0]
    slab_cols = block_size // replicas
    column = lax.axis_index("rep") * slab_cols
    own_cols = lax.dynamic_slice_in_dim(grad, column, slab_cols, 2)
    targets = jnp.arange(owners * capacity, dtype=jnp.int32)
    placing = (targets[:, None] == block_slot[None, :]).astype(jnp.bfloat16)
    packed = jnp.dot(
        placing, own_cols.reshape(blocks, band_rows * slab_cols), preferred_element_type=jnp.float32
    ).astype(jnp.bfloat16)
    packed = packed.reshape(owners, capacity, band_rows, slab_cols)
    arrived = lax.all_to_all(packed, "dp", split_axis=0, concat_axis=2, tiled=True)[0]
    gathered = lax.all_gather(arrived, "rep", axis=2, tiled=True)
    row_part = lax.dynamic_slice_in_dim(gathered, column, slab_cols, 1)
    left_term = jnp.einsum("sik,sjk->sij", row_part, gathered, preferred_element_type=jnp.float32)
    right_term = jnp.einsum("ski,skj->sij", arrived, gathered, preferred_element_type=jnp.float32)
    left_new = decay_rate * left_stat + (1.0 - decay_rate) * left_term
    right_new = decay_rate * right_stat + (1.0 - decay_rate) * right_term
    widened = gathered.astype(jnp.float32)
    graft_new = decay_rate * graft_acc + (1.0 - decay_rate) * widened * widened
    direction = widened / (jnp.sqrt(graft_new) + epsilon)
    graft_norm = jnp.sqrt(jnp.sum(direction * direction, axis=(1, 2)))
    middle = jnp.einsum(
        "sik,skj->sij", gathered, right_root, preferred_element_type=jnp.float32
    ).astype(jnp.bfloat16)
    full_precond = jnp.einsum("sik,skj->sij", left_root, middle, preferred_element_type=jnp.float32)
    squares = jnp.sum(full_precond * full_precond, axis=(1, 2))
    precond = lax.dynamic_slice_in_dim(full_precond, column, slab_cols, 2)
    graft_scale = graft_norm / (jnp.sqrt(squares) + epsilon)
    out_slab = (graft_scale[:, None, None] * precond).astype(jnp.bfloat16)
    returned = lax.all_to_all(out_slab[None], "dp", split_axis=2, concat_axis=0, tiled=True)
    spread = jnp.dot(
        placing.T,
        returned.reshape(owners * capacity, band_rows * slab_cols),
        preferred_element_type=jnp.float32,
    ).astype(jnp.bfloat16)
    update = spread.reshape(blocks, band_rows, slab_cols)
    return (update, left_new, right_new, graft_new)

def flipped(index, mask):
    bit = 1
    result = index
    while bit <= mask:
        if mask & bit:
            result = result + bit * (1 - 2 * ((index // bit) % 2))
        bit *= 2
    return result


def kernel(
    owners, replicas, slot_ref, grad_hbm, left_hbm, right_hbm, lroot_hbm, rroot_hbm, graft_hbm,
    update_ref, left, right, graft,
    own_grad, pack, placed, lroot, rroot, middle, precond, slab, returned,
    load_sem, send, recv1, recv_y, recv_c, recv3,
):
    me = lax.axis_index("dp")
    rep = lax.axis_index("rep")
    blocks, band, size = own_grad.shape
    capacity = placed.shape[0]
    slab_cols = slab.shape[2]
    peers = replicas // 2
    partner = flipped(rep, 1)

    def peer(j):
        return (rep + 2 * j) % replicas

    def cols_of(index):
        return pl.ds(pl.multiple_of(index * slab_cols, slab_cols), slab_cols)

    def rows_of(owner):
        return pl.ds(pl.multiple_of(owner * band, band), band)

    def remote(src, dst, ssem, rsem, device):
        return pltpu.make_async_remote_copy(
            src_ref=src, dst_ref=dst, send_sem=ssem, recv_sem=rsem,
            device_id=device, device_id_type=pl.DeviceIdType.MESH,
        )

    cols = cols_of(rep)
    barrier = pltpu.get_barrier_semaphore()
    others = [(flipped(me, k), rep) for k in range(1, owners)]
    others += [(me, partner)] + [(me, peer(j)) for j in range(1, peers)]
    for device in others:
        pl.semaphore_signal(barrier, inc=1, device_id=device, device_id_type=pl.DeviceIdType.MESH)

    grad_load = pltpu.make_async_copy(grad_hbm, own_grad, load_sem.at[0])
    grad_load.start()
    loads = []
    for n, (src, dst) in enumerate(
        ((graft_hbm, graft), (rroot_hbm, rroot), (lroot_hbm, lroot), (left_hbm, left), (right_hbm, right))
    ):
        loads.append(pltpu.make_async_copy(src, dst, load_sem.at[n + 1]))
        loads[n].start()

    grad_load.wait()
    def find(slot):
        block = jnp.int32(0)
        named = jnp.int32(0)
        for b in range(blocks):
            hit = slot_ref[b] == slot
            block = jnp.where(hit, b, block)
            named = jnp.where(hit, 1, named)
        return block, named > 0

    for s in range(owners * capacity):
        block, named = find(s)
        for j in range(peers):
            tile = own_grad[block, :, cols_of(peer(j))]
            pack[j, s // capacity, s % capacity] = jnp.where(named, tile, jnp.zeros_like(tile))
    for c in range(capacity):
        block, named = find(me * capacity + c)
        tile = own_grad[block]
        placed[c, rows_of(me), :] = jnp.where(named, tile, jnp.zeros_like(tile))

    pl.semaphore_wait(barrier, len(others))

    half = owners // 2
    far = sorted(range(half, owners), key=lambda k: (k % 2, k))
    near = list(range(1, half))
    sent = [0] * 4
    for c in range(capacity):
        for k in far + near:
            to = flipped(me, k)
            for j in range(peers if k < half else 1):
                copy = remote(
                    pack.at[j, to, c], placed.at[c, rows_of(me), cols_of(peer(j))],
                    send.at[0], recv1.at[c, k - 1], (to, rep),
                )
                copy.start()
                sent[0] += 1

    norms = [jnp.zeros((band // 4, size), jnp.float32) for _ in range(capacity)]
    squares = [jnp.zeros((1, 1), jnp.float32) for _ in range(capacity)]
    tasks = []

    def multiply(c, q):
        part = pl.ds(q * size, size)
        full = jnp.dot(lroot[c, part, :], middle[c], preferred_element_type=jnp.float32)
        precond[c, part, :] = full
        squares[c] = squares[c] + jnp.sum(full * full, axis=(0, 1), keepdims=True)

    def finish(c):
        graft_norm = jnp.sqrt(jnp.sum(norms[c], axis=(0, 1), keepdims=True))
        scale = graft_norm / (jnp.sqrt(squares[c]) + epsilon)
        slab[c] = (scale * precond[c, :, cols]).astype(jnp.bfloat16)
        mine = returned.at[me * capacity + c]
        for k in far + near:
            to = flipped(me, k)
            remote(slab.at[c, rows_of(to), :], mine, send.at[3], recv3.at[0], (to, rep)).start()
            sent[3] += 1
        returned[me * capacity + c] = slab[c, rows_of(me), :]

    def bytes_of(pieces, sem):
        rows = pieces * band * slab_cols // size
        view = placed.at[0, pl.ds(0, rows), :]
        return remote(view, view, sem, sem, (me, partner))

    def forward(c, k):
        bytes_of(peers if k < half else 1, recv1.at[c, k - 1]).wait_recv()
        rows = rows_of(flipped(me, k))
        if k >= half:
            piece = placed.at[c, rows, cols]
            for j in range(1, peers):
                remote(piece, piece, send.at[1], recv_y.at[j - 1, c, k - half], (me, peer(j))).start()
                sent[1] += 1
        for j in range(peers if k < half else 1):
            piece = placed.at[c, rows, cols_of(peer(j))]
            remote(piece, piece, send.at[2], recv_c.at[c, k - 1], (me, partner)).start()
            sent[2] += 1

    def relay(c, k):
        for j in range(1, peers):
            bytes_of(1, recv_y.at[j - 1, c, k - half]).wait_recv()
            theirs = (rep + replicas - 2 * j) % replicas
            piece = placed.at[c, rows_of(flipped(me, k)), cols_of(theirs)]
            remote(piece, piece, send.at[2], recv_c.at[c, k - 1], (me, partner)).start()
            sent[2] += 1

    def absorb(c, k):
        if k > 0:
            bytes_of(peers, recv_c.at[c, k - 1]).wait_recv()
        rows = rows_of(flipped(me, k))
        middle[c, rows, :] = jnp.dot(
            placed[c, rows, :], rroot[c], preferred_element_type=jnp.float32
        ).astype(jnp.bfloat16)
        for g in range(4):
            part = pl.ds(pl.multiple_of(flipped(me, k) * band + g * (band // 4), band // 4), band // 4)
            wide = placed[c, part, :].astype(jnp.float32)
            fresh = decay_rate * graft[c, part, :] + (1.0 - decay_rate) * wide * wide
            graft[c, part, :] = fresh
            direction = wide / (jnp.sqrt(fresh) + epsilon)
            norms[c] = norms[c] + direction * direction
        left_over[c] -= 1
        if left_over[c] == 0:
            tasks.extend(functools.partial(multiply, c, q) for q in range(1))
            tasks.append(functools.partial(finish, c))

    left_over = [owners] * capacity
    arrivals = near[:1] + far[:1] + near[1:2] + far[1:2] + near[2:] + far[2:]
    lag_y = 8
    lag_c = 5
    events = []
    for n, (c, k) in enumerate((c, k) for c in range(capacity) for k in arrivals):
        events.append((n, 0, forward, c, k))
        if k >= half:
            events.append((n + lag_y, 1, relay, c, k))
        events.append((n + lag_c + (lag_y if k >= half else 0), 2, absorb, c, k))
    events.sort(key=lambda event: event[:2])
    begun = 0
    for event in events:
        if event[2] is absorb and not begun:
            begun = 1
            for load in loads[:3]:
                load.wait()
            for c in range(capacity):
                absorb(c, 0)
        if tasks:
            tasks.pop(0)()
        event[2](*event[3:])
    for task in tasks:
        task()

    loads[3].wait()
    loads[4].wait()
    for c in range(capacity):
        term = lax.dot_general(
            placed[c, cols, :], placed[c], (((1,), (1,)), ((), ())), preferred_element_type=jnp.float32
        )
        left[c] = decay_rate * left[c] + (1.0 - decay_rate) * term
        term = lax.dot_general(
            placed[c, :, cols], placed[c], (((0,), (0,)), ((), ())), preferred_element_type=jnp.float32
        )
        right[c] = decay_rate * right[c] + (1.0 - decay_rate) * term

    bytes_of(sent[3], recv3.at[0]).wait_recv()
    for b in range(blocks):
        update_ref[b] = returned[slot_ref[b]]
    for stage, pieces in enumerate(sent):
        bytes_of(pieces, send.at[stage]).wait_send()


def write_out(*refs):
    n = (len(refs) - 1) // 2
    sem = refs[-1]
    copies = [pltpu.make_async_copy(refs[i], refs[n + i], sem.at[i]) for i in range(n)]
    for copy in copies:
        copy.start()
    for copy in copies:
        copy.wait()


def local(grad, block_slot, left_stat, right_stat, left_root, right_root, graft_acc):
    owners = lax.axis_size("dp")
    replicas = lax.axis_size("rep")
    blocks, band, size = grad.shape
    capacity = left_stat.shape[0]
    slab_cols = size // replicas
    power_of_two = owners & (owners - 1) == 0 and owners >= 4
    if slab_cols % 128 or band % 64 or replicas % 2 or not power_of_two:
        return local_plain(grad, block_slot, left_stat, right_stat, left_root, right_root, graft_acc)
    peers = replicas // 2
    slots = owners * capacity
    f32, bf16 = jnp.float32, jnp.bfloat16
    vmem = pltpu.VMEM
    dma = pltpu.SemaphoreType.DMA
    anywhere = pl.BlockSpec(memory_space=pltpu.HBM)
    inside = pl.BlockSpec(memory_space=vmem)
    results = (
        ((blocks, band, slab_cols), bf16),
        (left_stat.shape, f32),
        (right_stat.shape, f32),
        (graft_acc.shape, f32),
    )
    held = pl.pallas_call(
        functools.partial(kernel, owners, replicas),
        out_shape=tuple(vmem(*r) for r in results),
        in_specs=[pl.BlockSpec(memory_space=pltpu.SMEM)] + [anywhere] * 6,
        out_specs=(inside,) * 4,
        scratch_shapes=[
            vmem((blocks, band, size), bf16),
            vmem((peers, owners, capacity, band, slab_cols), bf16),
            vmem((capacity, size, size), bf16),
            vmem(left_root.shape, bf16),
            vmem(right_root.shape, bf16),
            vmem((capacity, size, size), bf16),
            vmem((capacity, size, size), f32),
            vmem((capacity, size, slab_cols), bf16),
            vmem((slots, band, slab_cols), bf16),
            dma((6,)),
            dma((4,)),
            dma((capacity, owners - 1)),
            dma((peers - 1, capacity, owners // 2)),
            dma((capacity, owners - 1)),
            dma((1,)),
        ],
        compiler_params=pltpu.CompilerParams(
            collective_id=0, has_side_effects=True, vmem_limit_bytes=60 * 1024 * 1024
        ),
    )(block_slot, grad, left_stat, right_stat, left_root, right_root, graft_acc)
    return pl.pallas_call(
        write_out,
        out_shape=tuple(jax.ShapeDtypeStruct(*r) for r in results),
        in_specs=[inside] * 4,
        out_specs=(anywhere,) * 4,
        scratch_shapes=[dma((4,))],
        compiler_params=pltpu.CompilerParams(vmem_limit_bytes=16 * 1024 * 1024),
    )(*held)


def solution(mesh):
    return jax.shard_map(
        local,
        mesh=mesh,
        in_specs=(
            P(None, "dp", None),
            P(),
            P("dp", "rep", None),
            P("dp", "rep", None),
            P("dp", None, None),
            P("dp", None, None),
            P("dp", None, None),
        ),
        out_specs=(
            P(None, "dp", "rep"),
            P("dp", "rep", None),
            P("dp", "rep", None),
            P("dp", None, None),
        ),
        check_vma=False,
    )
```

```python
import functools

import jax
import jax.numpy as jnp
from jax import lax
from jax.experimental import pallas as pl
from jax.experimental.pallas import tpu as pltpu
from jax.sharding import PartitionSpec as P

decay_rate = 0.99
epsilon = 1e-06


def local_plain(grad, block_slot, left_stat, right_stat, left_root, right_root, graft_acc):
    owners = lax.axis_size("dp")
    replicas = lax.axis_size("rep")
    blocks, band_rows, block_size = grad.shape
    capacity = left_stat.shape[0]
    slab_cols = block_size // replicas
    column = lax.axis_index("rep") * slab_cols
    own_cols = lax.dynamic_slice_in_dim(grad, column, slab_cols, 2)
    targets = jnp.arange(owners * capacity, dtype=jnp.int32)
    placing = (targets[:, None] == block_slot[None, :]).astype(jnp.bfloat16)
    packed = jnp.dot(
        placing, own_cols.reshape(blocks, band_rows * slab_cols), preferred_element_type=jnp.float32
    ).astype(jnp.bfloat16)
    packed = packed.reshape(owners, capacity, band_rows, slab_cols)
    arrived = lax.all_to_all(packed, "dp", split_axis=0, concat_axis=2, tiled=True)[0]
    gathered = lax.all_gather(arrived, "rep", axis=2, tiled=True)
    row_part = lax.dynamic_slice_in_dim(gathered, column, slab_cols, 1)
    left_term = jnp.einsum("sik,sjk->sij", row_part, gathered, preferred_element_type=jnp.float32)
    right_term = jnp.einsum("ski,skj->sij", arrived, gathered, preferred_element_type=jnp.float32)
    left_new = decay_rate * left_stat + (1.0 - decay_rate) * left_term
    right_new = decay_rate * right_stat + (1.0 - decay_rate) * right_term
    widened = gathered.astype(jnp.float32)
    graft_new = decay_rate * graft_acc + (1.0 - decay_rate) * widened * widened
    direction = widened / (jnp.sqrt(graft_new) + epsilon)
    graft_norm = jnp.sqrt(jnp.sum(direction * direction, axis=(1, 2)))
    middle = jnp.einsum(
        "sik,skj->sij", gathered, right_root, preferred_element_type=jnp.float32
    ).astype(jnp.bfloat16)
    full_precond = jnp.einsum("sik,skj->sij", left_root, middle, preferred_element_type=jnp.float32)
    squares = jnp.sum(full_precond * full_precond, axis=(1, 2))
    precond = lax.dynamic_slice_in_dim(full_precond, column, slab_cols, 2)
    graft_scale = graft_norm / (jnp.sqrt(squares) + epsilon)
    out_slab = (graft_scale[:, None, None] * precond).astype(jnp.bfloat16)
    returned = lax.all_to_all(out_slab[None], "dp", split_axis=2, concat_axis=0, tiled=True)
    spread = jnp.dot(
        placing.T,
        returned.reshape(owners * capacity, band_rows * slab_cols),
        preferred_element_type=jnp.float32,
    ).astype(jnp.bfloat16)
    update = spread.reshape(blocks, band_rows, slab_cols)
    return (update, left_new, right_new, graft_new)

def flipped(index, mask):
    bit = 1
    result = index
    while bit <= mask:
        if mask & bit:
            result = result + bit * (1 - 2 * ((index // bit) % 2))
        bit *= 2
    return result


def kernel(
    owners, replicas, slot_hbm, grad_hbm, left_hbm, right_hbm, lroot_hbm, rroot_hbm, graft_hbm,
    update_ref, left, right, graft,
    slot_ref, own_grad, pack, placed, lroot, rroot, norm_parts, precond, slab, returned,
    load_sem, send, recv1, recv_y, recv_c, recv_n, recv3,
):
    me = lax.axis_index("dp")
    rep = lax.axis_index("rep")
    blocks, band, size = own_grad.shape
    capacity = placed.shape[0]
    slab_cols = slab.shape[2]
    peers = replicas // 2
    partner = flipped(rep, 1)

    def peer(j):
        return (rep + 2 * j) % replicas

    def cols_of(index):
        return pl.ds(pl.multiple_of(index * slab_cols, slab_cols), slab_cols)

    def rows_of(owner):
        return pl.ds(pl.multiple_of(owner * band, band), band)

    def remote(src, dst, ssem, rsem, device):
        return pltpu.make_async_remote_copy(
            src_ref=src, dst_ref=dst, send_sem=ssem, recv_sem=rsem,
            device_id=device, device_id_type=pl.DeviceIdType.MESH,
        )

    grad_load = pltpu.make_async_copy(grad_hbm, own_grad, load_sem.at[0])
    grad_load.start()
    slot_load = pltpu.make_async_copy(slot_hbm, slot_ref, load_sem.at[6])
    slot_load.start()
    cols = cols_of(rep)
    barrier = pltpu.get_barrier_semaphore()
    others = [(flipped(me, k), rep) for k in range(1, owners)]
    group = [(me, (rep + j) % replicas) for j in range(1, replicas)]
    others += group
    for device in others:
        pl.semaphore_signal(barrier, inc=1, device_id=device, device_id_type=pl.DeviceIdType.MESH)

    loads = []
    for n, (src, dst) in enumerate(
        ((graft_hbm, graft), (rroot_hbm, rroot), (lroot_hbm, lroot), (left_hbm, left), (right_hbm, right))
    ):
        loads.append(pltpu.make_async_copy(src, dst, load_sem.at[n + 1]))
        loads[n].start()

    slot_load.wait()
    grad_load.wait()
    def find(slot):
        block = jnp.int32(0)
        named = jnp.int32(0)
        for b in range(blocks):
            hit = slot_ref[b] == slot
            block = jnp.where(hit, b, block)
            named = jnp.where(hit, 1, named)
        return block, named > 0

    for s in range(owners * capacity):
        block, named = find(s)
        for j in range(peers):
            tile = own_grad[block, :, cols_of(peer(j))]
            pack[j, s // capacity, s % capacity] = jnp.where(named, tile, jnp.zeros_like(tile))
    for c in range(capacity):
        block, named = find(me * capacity + c)
        tile = own_grad[block]
        placed[c, rows_of(me), :] = jnp.where(named, tile, jnp.zeros_like(tile))

    pl.semaphore_wait(barrier, len(others))

    half = owners // 2
    far = sorted(range(half, owners), key=lambda k: (k % 2, k))
    near = list(range(1, half))
    sent = [0] * 5
    for c in range(capacity):
        for k in far + near:
            to = flipped(me, k)
            for j in range(peers if k < half else 1):
                copy = remote(
                    pack.at[j, to, c], placed.at[c, rows_of(me), cols_of(peer(j))],
                    send.at[0], recv1.at[c, k - 1], (to, rep),
                )
                copy.start()
                sent[0] += 1

    def bytes_of(pieces, sem):
        rows = pieces * band * slab_cols // size
        view = placed.at[0, pl.ds(0, rows), :]
        return remote(view, view, sem, sem, (me, partner))

    def forward(c, k):
        bytes_of(peers if k < half else 1, recv1.at[c, k - 1]).wait_recv()
        rows = rows_of(flipped(me, k))
        if k >= half:
            piece = placed.at[c, rows, cols]
            for j in range(1, peers):
                remote(piece, piece, send.at[1], recv_y.at[j - 1, c, k - half], (me, peer(j))).start()
                sent[1] += 1
        for j in range(peers if k < half else 1):
            piece = placed.at[c, rows, cols_of(peer(j))]
            remote(piece, piece, send.at[2], recv_c.at[c, k // half], (me, partner)).start()
            sent[2] += 1

    def relay(c, k):
        for j in range(1, peers):
            bytes_of(1, recv_y.at[j - 1, c, k - half]).wait_recv()
            theirs = (rep + replicas - 2 * j) % replicas
            piece = placed.at[c, rows_of(flipped(me, k)), cols_of(theirs)]
            remote(piece, piece, send.at[2], recv_c.at[c, k // half], (me, partner)).start()
            sent[2] += 1

    norms = [jnp.zeros((8, slab_cols), jnp.float32) for _ in range(capacity)]

    def measure(c, k):
        rows = rows_of(flipped(me, k))
        wide = placed[c, rows, cols].astype(jnp.float32)
        fresh = decay_rate * graft[c, rows, cols] + (1.0 - decay_rate) * wide * wide
        direction = wide / (jnp.sqrt(fresh) + epsilon)
        norms[c] = norms[c] + jnp.sum((direction * direction).reshape(band // 8, 8, slab_cols), axis=0)

    def share(c):
        norm_parts[c * replicas + rep] = norms[c]
        mine = norm_parts.at[c * replicas + rep]
        for device in group:
            remote(mine, mine, send.at[4], recv_n.at[c], device).start()
            sent[4] += 1

    def tiles_of(count, sem):
        view = norm_parts.at[pl.ds(0, count)]
        return remote(view, view, sem, sem, (me, partner))

    def half_rows(side):
        start = (me // half + side) % 2
        return pl.ds(pl.multiple_of(start * half * band, half * band), half * band)

    def product(c, side):
        rows = half_rows(side)
        middle = jnp.dot(
            placed[c, rows, :], rroot[c], preferred_element_type=jnp.float32
        ).astype(jnp.bfloat16)
        return jnp.dot(lroot[c, :, rows], middle, preferred_element_type=jnp.float32)

    def begin(c):
        bytes_of(peers * (half - 1), recv_c.at[c, 0]).wait_recv()
        precond[c] = product(c, 0)

    def complete(c):
        bytes_of(peers * half, recv_c.at[c, 1]).wait_recv()
        full = precond[c] + product(c, 1)
        precond[c] = full
        squares = jnp.sum(full * full, axis=(0, 1), keepdims=True)
        tiles_of(replicas - 1, recv_n.at[c]).wait_recv()
        total = jnp.sum(norm_parts[pl.ds(c * replicas, replicas)], axis=0)
        graft_norm = jnp.sqrt(jnp.sum(total, axis=(0, 1), keepdims=True))
        scale = graft_norm / (jnp.sqrt(squares) + epsilon)
        slab[c] = (scale * precond[c, :, cols]).astype(jnp.bfloat16)
        mine = returned.at[me * capacity + c]
        for k in far + near:
            to = flipped(me, k)
            remote(slab.at[c, rows_of(to), :], mine, send.at[3], recv3.at[0], (to, rep)).start()
            sent[3] += 1
        returned[me * capacity + c] = slab[c, rows_of(me), :]

    for load in loads[:3]:
        load.wait()
    for c in range(capacity):
        measure(c, 0)
    plan = [('f', 0, 1), ('f', 0, 4), ('f', 0, 2), ('f', 0, 6), ('f', 0, 5), ('f', 0, 7), ('f', 0, 3), ('n', 0, 0), ('f', 1, 4), ('f', 1, 1), ('r', 0, 4), ('f', 1, 6), ('f', 1, 2), ('r', 0, 6), ('f', 1, 5), ('f', 1, 7), ('f', 1, 3), ('n', 1, 0), ('b', 0, 0), ('r', 0, 5), ('r', 0, 7), ('r', 1, 4), ('r', 1, 6), ('c', 0, 0), ('r', 1, 5), ('r', 1, 7), ('b', 1, 0), ('c', 1, 0)]
    for name, c, k in plan:
        if name == "f":
            forward(c, k)
            measure(c, k)
        elif name == "r":
            relay(c, k)
        else:
            {"n": share, "b": begin, "c": complete}[name](c)

    loads[3].wait()
    loads[4].wait()
    for c in range(capacity):
        for g in range(owners):
            part = pl.ds(g * band, band)
            wide = placed[c, part, :].astype(jnp.float32)
            graft[c, part, :] = decay_rate * graft[c, part, :] + (1.0 - decay_rate) * wide * wide
    for c in range(capacity):
        term = lax.dot_general(
            placed[c, cols, :], placed[c], (((1,), (1,)), ((), ())), preferred_element_type=jnp.float32
        )
        left[c] = decay_rate * left[c] + (1.0 - decay_rate) * term
        term = lax.dot_general(
            placed[c, :, cols], placed[c], (((0,), (0,)), ((), ())), preferred_element_type=jnp.float32
        )
        right[c] = decay_rate * right[c] + (1.0 - decay_rate) * term

    bytes_of(sent[3], recv3.at[0]).wait_recv()
    for b in range(blocks):
        update_ref[b] = returned[slot_ref[b]]
    for stage, pieces in enumerate(sent[:4]):
        bytes_of(pieces, send.at[stage]).wait_send()
    tiles_of(sent[4], send.at[4]).wait_send()


def write_out(*refs):
    n = (len(refs) - 1) // 2
    sem = refs[-1]
    copies = [pltpu.make_async_copy(refs[i], refs[n + i], sem.at[i]) for i in range(n)]
    for copy in copies:
        copy.start()
    for copy in copies:
        copy.wait()


def local(grad, block_slot, left_stat, right_stat, left_root, right_root, graft_acc):
    owners = lax.axis_size("dp")
    replicas = lax.axis_size("rep")
    blocks, band, size = grad.shape
    capacity = left_stat.shape[0]
    slab_cols = size // replicas
    power_of_two = owners & (owners - 1) == 0 and owners >= 4
    if slab_cols % 128 or band % 64 or replicas % 2 or not power_of_two:
        return local_plain(grad, block_slot, left_stat, right_stat, left_root, right_root, graft_acc)
    peers = replicas // 2
    slots = owners * capacity
    f32, bf16 = jnp.float32, jnp.bfloat16
    vmem = pltpu.VMEM
    dma = pltpu.SemaphoreType.DMA
    anywhere = pl.BlockSpec(memory_space=pltpu.HBM)
    inside = pl.BlockSpec(memory_space=vmem)
    results = (
        ((blocks, band, slab_cols), bf16),
        (left_stat.shape, f32),
        (right_stat.shape, f32),
        (graft_acc.shape, f32),
    )
    held = pl.pallas_call(
        functools.partial(kernel, owners, replicas),
        out_shape=tuple(vmem(*r) for r in results),
        in_specs=[anywhere] * 7,
        out_specs=(inside,) * 4,
        scratch_shapes=[
            pltpu.SMEM(block_slot.shape, jnp.int32),
            vmem((blocks, band, size), bf16),
            vmem((peers, owners, capacity, band, slab_cols), bf16),
            vmem((capacity, size, size), bf16),
            vmem(left_root.shape, bf16),
            vmem(right_root.shape, bf16),
            vmem((capacity * replicas, 8, slab_cols), f32),
            vmem((capacity, size, size), f32),
            vmem((capacity, size, slab_cols), bf16),
            vmem((slots, band, slab_cols), bf16),
            dma((7,)),
            dma((5,)),
            dma((capacity, owners - 1)),
            dma((peers - 1, capacity, owners // 2)),
            dma((capacity, 2)),
            dma((capacity,)),
            dma((1,)),
        ],
        compiler_params=pltpu.CompilerParams(
            collective_id=0, has_side_effects=True, vmem_limit_bytes=60 * 1024 * 1024
        ),
    )(block_slot, grad, left_stat, right_stat, left_root, right_root, graft_acc)
    return pl.pallas_call(
        write_out,
        out_shape=tuple(jax.ShapeDtypeStruct(*r) for r in results),
        in_specs=[inside] * 4,
        out_specs=(anywhere,) * 4,
        scratch_shapes=[dma((4,))],
        compiler_params=pltpu.CompilerParams(vmem_limit_bytes=16 * 1024 * 1024),
    )(*held)


def solution(mesh):
    return jax.shard_map(
        local,
        mesh=mesh,
        in_specs=(
            P(None, "dp", None),
            P(),
            P("dp", "rep", None),
            P("dp", "rep", None),
            P("dp", None, None),
            P("dp", None, None),
            P("dp", None, None),
        ),
        out_specs=(
            P(None, "dp", "rep"),
            P("dp", "rep", None),
            P("dp", "rep", None),
            P("dp", None, None),
        ),
        check_vma=False,
    )
```

```python
import functools

import jax
import jax.numpy as jnp
from jax import lax
from jax.experimental import pallas as pl
from jax.experimental.pallas import tpu as pltpu
from jax.sharding import PartitionSpec as P

decay_rate = 0.99
epsilon = 1e-06


def local_plain(grad, block_slot, left_stat, right_stat, left_root, right_root, graft_acc):
    owners = lax.axis_size("dp")
    replicas = lax.axis_size("rep")
    blocks, band_rows, block_size = grad.shape
    capacity = left_stat.shape[0]
    slab_cols = block_size // replicas
    column = lax.axis_index("rep") * slab_cols
    own_cols = lax.dynamic_slice_in_dim(grad, column, slab_cols, 2)
    targets = jnp.arange(owners * capacity, dtype=jnp.int32)
    placing = (targets[:, None] == block_slot[None, :]).astype(jnp.bfloat16)
    packed = jnp.dot(
        placing, own_cols.reshape(blocks, band_rows * slab_cols), preferred_element_type=jnp.float32
    ).astype(jnp.bfloat16)
    packed = packed.reshape(owners, capacity, band_rows, slab_cols)
    arrived = lax.all_to_all(packed, "dp", split_axis=0, concat_axis=2, tiled=True)[0]
    gathered = lax.all_gather(arrived, "rep", axis=2, tiled=True)
    row_part = lax.dynamic_slice_in_dim(gathered, column, slab_cols, 1)
    left_term = jnp.einsum("sik,sjk->sij", row_part, gathered, preferred_element_type=jnp.float32)
    right_term = jnp.einsum("ski,skj->sij", arrived, gathered, preferred_element_type=jnp.float32)
    left_new = decay_rate * left_stat + (1.0 - decay_rate) * left_term
    right_new = decay_rate * right_stat + (1.0 - decay_rate) * right_term
    widened = gathered.astype(jnp.float32)
    graft_new = decay_rate * graft_acc + (1.0 - decay_rate) * widened * widened
    direction = widened / (jnp.sqrt(graft_new) + epsilon)
    graft_norm = jnp.sqrt(jnp.sum(direction * direction, axis=(1, 2)))
    middle = jnp.einsum(
        "sik,skj->sij", gathered, right_root, preferred_element_type=jnp.float32
    ).astype(jnp.bfloat16)
    full_precond = jnp.einsum("sik,skj->sij", left_root, middle, preferred_element_type=jnp.float32)
    squares = jnp.sum(full_precond * full_precond, axis=(1, 2))
    precond = lax.dynamic_slice_in_dim(full_precond, column, slab_cols, 2)
    graft_scale = graft_norm / (jnp.sqrt(squares) + epsilon)
    out_slab = (graft_scale[:, None, None] * precond).astype(jnp.bfloat16)
    returned = lax.all_to_all(out_slab[None], "dp", split_axis=2, concat_axis=0, tiled=True)
    spread = jnp.dot(
        placing.T,
        returned.reshape(owners * capacity, band_rows * slab_cols),
        preferred_element_type=jnp.float32,
    ).astype(jnp.bfloat16)
    update = spread.reshape(blocks, band_rows, slab_cols)
    return (update, left_new, right_new, graft_new)

def flipped(index, mask):
    bit = 1
    result = index
    while bit <= mask:
        if mask & bit:
            result = result + bit * (1 - 2 * ((index // bit) % 2))
        bit *= 2
    return result


def kernel(
    owners, replicas, slot_hbm, grad_hbm, left_hbm, right_hbm, lroot_hbm, rroot_hbm, graft_hbm,
    update_ref, left, right, graft,
    slot_ref, own_grad, pack, placed, lroot, rroot, norm_parts, precond, slab, returned,
    load_sem, send, recv1, recv_y, recv_c, recv_n, recv3,
):
    me = lax.axis_index("dp")
    rep = lax.axis_index("rep")
    blocks, band, size = own_grad.shape
    capacity = placed.shape[0]
    slab_cols = slab.shape[2]
    peers = replicas // 2
    partner = flipped(rep, 1)

    def peer(j):
        return (rep + 2 * j) % replicas

    def cols_of(index):
        return pl.ds(pl.multiple_of(index * slab_cols, slab_cols), slab_cols)

    def rows_of(owner):
        return pl.ds(pl.multiple_of(owner * band, band), band)

    def remote(src, dst, ssem, rsem, device):
        return pltpu.make_async_remote_copy(
            src_ref=src, dst_ref=dst, send_sem=ssem, recv_sem=rsem,
            device_id=device, device_id_type=pl.DeviceIdType.MESH,
        )

    grad_load = pltpu.make_async_copy(grad_hbm, own_grad, load_sem.at[0])
    grad_load.start()
    slot_load = pltpu.make_async_copy(slot_hbm, slot_ref, load_sem.at[6])
    slot_load.start()
    cols = cols_of(rep)
    barrier = pltpu.get_barrier_semaphore()
    others = [(flipped(me, k), rep) for k in reversed(range(1, owners))]
    group = [(me, (rep + j) % replicas) for j in range(1, replicas)]
    others += group
    for device in others:
        pl.semaphore_signal(barrier, inc=1, device_id=device, device_id_type=pl.DeviceIdType.MESH)

    loads = []
    for n, (src, dst) in enumerate(
        ((graft_hbm, graft), (rroot_hbm, rroot), (lroot_hbm, lroot), (left_hbm, left), (right_hbm, right))
    ):
        loads.append(pltpu.make_async_copy(src, dst, load_sem.at[n + 1]))
        loads[n].start()

    slot_load.wait()
    grad_load.wait()
    def find(slot):
        block = jnp.int32(0)
        named = jnp.int32(0)
        for b in range(blocks):
            hit = slot_ref[b] == slot
            block = jnp.where(hit, b, block)
            named = jnp.where(hit, 1, named)
        return block, named > 0

    for s in range(owners * capacity):
        block, named = find(s)
        for j in range(peers):
            tile = own_grad[block, :, cols_of(peer(j))]
            pack[j, s // capacity, s % capacity] = jnp.where(named, tile, jnp.zeros_like(tile))
    for c in range(capacity):
        block, named = find(me * capacity + c)
        tile = own_grad[block]
        placed[c, rows_of(me), :] = jnp.where(named, tile, jnp.zeros_like(tile))

    pl.semaphore_wait(barrier, len(others))

    half = owners // 2
    far = list(reversed(range(half, owners)))
    near = list(range(1, half))
    sent = [0] * 5
    for c in range(capacity):
        for k in far + near:
            to = flipped(me, k)
            for j in range(peers if k < half else 1):
                copy = remote(
                    pack.at[j, to, c], placed.at[c, rows_of(me), cols_of(peer(j))],
                    send.at[0], recv1.at[c, k - 1], (to, rep),
                )
                copy.start()
                sent[0] += 1

    def bytes_of(pieces, sem):
        rows = pieces * band * slab_cols // size
        view = placed.at[0, pl.ds(0, rows), :]
        return remote(view, view, sem, sem, (me, partner))

    def forward(c, k):
        bytes_of(peers if k < half else 1, recv1.at[c, k - 1]).wait_recv()
        rows = rows_of(flipped(me, k))
        if k >= half:
            piece = placed.at[c, rows, cols]
            for j in range(1, peers):
                remote(piece, piece, send.at[1], recv_y.at[j - 1, c, k - half], (me, peer(j))).start()
                sent[1] += 1
        for j in range(peers if k < half else 1):
            piece = placed.at[c, rows, cols_of(peer(j))]
            remote(piece, piece, send.at[2], recv_c.at[c, k // half], (me, partner)).start()
            sent[2] += 1

    def relay(c, k):
        for j in range(1, peers):
            bytes_of(1, recv_y.at[j - 1, c, k - half]).wait_recv()
            theirs = (rep + replicas - 2 * j) % replicas
            piece = placed.at[c, rows_of(flipped(me, k)), cols_of(theirs)]
            remote(piece, piece, send.at[2], recv_c.at[c, k // half], (me, partner)).start()
            sent[2] += 1

    norms = [jnp.zeros((8, slab_cols), jnp.float32) for _ in range(capacity)]

    def measure(c, k):
        rows = rows_of(flipped(me, k))
        wide = placed[c, rows, cols].astype(jnp.float32)
        fresh = decay_rate * graft[c, rows, cols] + (1.0 - decay_rate) * wide * wide
        direction = wide / (jnp.sqrt(fresh) + epsilon)
        norms[c] = norms[c] + jnp.sum((direction * direction).reshape(band // 8, 8, slab_cols), axis=0)

    def share(c):
        norm_parts[c * replicas + rep] = norms[c]
        mine = norm_parts.at[c * replicas + rep]
        for device in group:
            remote(mine, mine, send.at[4], recv_n.at[c], device).start()
            sent[4] += 1

    def tiles_of(count, sem):
        view = norm_parts.at[pl.ds(0, count)]
        return remote(view, view, sem, sem, (me, partner))

    def half_rows(side):
        start = (me // half + side) % 2
        return pl.ds(pl.multiple_of(start * half * band, half * band), half * band)

    def product(c, side):
        rows = half_rows(side)
        middle = jnp.dot(
            placed[c, rows, :], rroot[c], preferred_element_type=jnp.float32
        ).astype(jnp.bfloat16)
        return jnp.dot(lroot[c, :, rows], middle, preferred_element_type=jnp.float32)

    def begin(c):
        bytes_of(peers * (half - 1), recv_c.at[c, 0]).wait_recv()
        precond[c] = product(c, 0)

    def complete(c):
        bytes_of(peers * half, recv_c.at[c, 1]).wait_recv()
        rows = half_rows(1)
        middle = jnp.dot(
            placed[c, rows, :], rroot[c], preferred_element_type=jnp.float32
        ).astype(jnp.bfloat16)
        folded = jnp.zeros((8, size), jnp.float32)
        step = size // 4
        for q in range(4):
            part = pl.ds(q * step, step)
            full = precond[c, part, :] + jnp.dot(lroot[c, part, rows], middle, preferred_element_type=jnp.float32)
            precond[c, part, :] = full
            folded = folded + jnp.sum((full * full).reshape(step // 8, 8, size), axis=0)
        squares = jnp.sum(folded, axis=(0, 1), keepdims=True)
        tiles_of(replicas - 1, recv_n.at[c]).wait_recv()
        total = jnp.sum(norm_parts[pl.ds(c * replicas, replicas)], axis=0)
        graft_norm = jnp.sqrt(jnp.sum(total, axis=(0, 1), keepdims=True))
        scale = graft_norm / (jnp.sqrt(squares) + epsilon)
        slab[c] = (scale * precond[c, :, cols]).astype(jnp.bfloat16)
        mine = returned.at[me * capacity + c]
        for k in far + near:
            to = flipped(me, k)
            remote(slab.at[c, rows_of(to), :], mine, send.at[3], recv3.at[0], (to, rep)).start()
            sent[3] += 1
        returned[me * capacity + c] = slab[c, rows_of(me), :]

    for load in loads[:3]:
        load.wait()
    for c in range(capacity):
        measure(c, 0)
    ahead = far[: half // 2]
    order = near[:1] + ahead + near[1:2] + far[half // 2 :] + near[2:]
    plan = [("f", 0, k) for k in order] + [("n", 0, 0)]
    for c in range(1, capacity):
        for n, k in enumerate(far):
            plan.append(("f", c, k))
            if n % 2:
                plan.append(("r", c - 1, far[n // 2]))
        plan += [("f", c, k) for k in near] + [("n", c, 0), ("b", c - 1, 0)]
        plan += [("r", c - 1, k) for k in far[half // 2 :]] + [("c", c - 1, 0)]
    plan += [("r", capacity - 1, k) for k in far]
    plan += [("b", capacity - 1, 0), ("c", capacity - 1, 0)]
    for name, c, k in plan:
        if name == "f":
            forward(c, k)
            measure(c, k)
        elif name == "r":
            relay(c, k)
        else:
            {"n": share, "b": begin, "c": complete}[name](c)

    loads[3].wait()
    loads[4].wait()
    for c in range(capacity):
        for g in range(owners):
            part = pl.ds(g * band, band)
            wide = placed[c, part, :].astype(jnp.float32)
            graft[c, part, :] = decay_rate * graft[c, part, :] + (1.0 - decay_rate) * wide * wide
    for c in range(capacity):
        term = lax.dot_general(
            placed[c, cols, :], placed[c], (((1,), (1,)), ((), ())), preferred_element_type=jnp.float32
        )
        left[c] = decay_rate * left[c] + (1.0 - decay_rate) * term
        term = lax.dot_general(
            placed[c, :, cols], placed[c], (((0,), (0,)), ((), ())), preferred_element_type=jnp.float32
        )
        right[c] = decay_rate * right[c] + (1.0 - decay_rate) * term

    bytes_of(sent[3], recv3.at[0]).wait_recv()
    for b in range(blocks):
        update_ref[b] = returned[slot_ref[b]]
    for stage, pieces in enumerate(sent[:4]):
        bytes_of(pieces, send.at[stage]).wait_send()
    tiles_of(sent[4], send.at[4]).wait_send()


def write_out(*refs):
    n = (len(refs) - 1) // 2
    sem = refs[-1]
    copies = [pltpu.make_async_copy(refs[i], refs[n + i], sem.at[i]) for i in range(n)]
    for copy in copies:
        copy.start()
    for copy in copies:
        copy.wait()


def local(grad, block_slot, left_stat, right_stat, left_root, right_root, graft_acc):
    owners = lax.axis_size("dp")
    replicas = lax.axis_size("rep")
    blocks, band, size = grad.shape
    capacity = left_stat.shape[0]
    slab_cols = size // replicas
    power_of_two = owners & (owners - 1) == 0 and owners >= 4
    fits = capacity * (owners - 1) * band <= 2 * size
    if slab_cols % 128 or band % 64 or replicas % 2 or not power_of_two or not fits:
        return local_plain(grad, block_slot, left_stat, right_stat, left_root, right_root, graft_acc)
    peers = replicas // 2
    slots = owners * capacity
    f32, bf16 = jnp.float32, jnp.bfloat16
    vmem = pltpu.VMEM
    dma = pltpu.SemaphoreType.DMA
    anywhere = pl.BlockSpec(memory_space=pltpu.HBM)
    inside = pl.BlockSpec(memory_space=vmem)
    results = (
        ((blocks, band, slab_cols), bf16),
        (left_stat.shape, f32),
        (right_stat.shape, f32),
        (graft_acc.shape, f32),
    )
    held = pl.pallas_call(
        functools.partial(kernel, owners, replicas),
        out_shape=tuple(vmem(*r) for r in results),
        in_specs=[anywhere] * 7,
        out_specs=(inside,) * 4,
        scratch_shapes=[
            pltpu.SMEM(block_slot.shape, jnp.int32),
            vmem((blocks, band, size), bf16),
            vmem((peers, owners, capacity, band, slab_cols), bf16),
            vmem((capacity, size, size), bf16),
            vmem(left_root.shape, bf16),
            vmem(right_root.shape, bf16),
            vmem((capacity * replicas, 8, slab_cols), f32),
            vmem((capacity, size, size), f32),
            vmem((capacity, size, slab_cols), bf16),
            vmem((slots, band, slab_cols), bf16),
            dma((7,)),
            dma((5,)),
            dma((capacity, owners - 1)),
            dma((peers - 1, capacity, owners // 2)),
            dma((capacity, 2)),
            dma((capacity,)),
            dma((1,)),
        ],
        compiler_params=pltpu.CompilerParams(
            collective_id=0, has_side_effects=True, vmem_limit_bytes=60 * 1024 * 1024
        ),
    )(block_slot, grad, left_stat, right_stat, left_root, right_root, graft_acc)
    return pl.pallas_call(
        write_out,
        out_shape=tuple(jax.ShapeDtypeStruct(*r) for r in results),
        in_specs=[inside] * 4,
        out_specs=(anywhere,) * 4,
        scratch_shapes=[dma((4,))],
        compiler_params=pltpu.CompilerParams(vmem_limit_bytes=16 * 1024 * 1024),
    )(*held)


def solution(mesh):
    return jax.shard_map(
        local,
        mesh=mesh,
        in_specs=(
            P(None, "dp", None),
            P(),
            P("dp", "rep", None),
            P("dp", "rep", None),
            P("dp", None, None),
            P("dp", None, None),
            P("dp", None, None),
        ),
        out_specs=(
            P(None, "dp", "rep"),
            P("dp", "rep", None),
            P("dp", "rep", None),
            P("dp", None, None),
        ),
        check_vma=False,
    )
```
